32 devices in a mesh: atom: 16 (over z, x, core), chan: 2 (over y).
Axes of the slice: x: 2, y: 2, z: 4, core: 2. Of those that a mesh axis runs over, the one named last changes fastest.
Arguments:
- positions: float32 [3, 2048], P(None, 'atom'), may hold values from -9 to 9
- features: bfloat16 [512, 2048], P('chan', 'atom'), may hold values from -6 to 6
- struct_ids: int32 [2048], P('atom'), may hold values from 0 to 15, as said below
- slots: int32 [64, 2048], P(None, 'atom'), may hold values from 0 to 96, as said below
- validity: int32 [64, 2048], P(None, 'atom'), may hold values from 0 to 1, as said below
- radial_in: bfloat16 [512, 128], replicated, may hold values from -72 to 72
- radial_out: bfloat16 [512, 512], P('chan'), may hold values from -0.0234375 to 0.0234375
- mixing: bfloat16 [512, 512], P(None, 'chan'), may hold values from -0.5 to 0.5
- readout: float32 [512], replicated, may hold values from -0.0078125 to 0.0078125
Outputs:
- forces: float32 [3, 2048], P(None, 'atom')
- stress: float32 [9, 16], replicated
The draws below stay inside these ranges and needn't reach their ends.
Inputs may be any that keep to these rules, and one draw needn't show every extreme that they name: `struct_ids`: structure numbers never fall along the atoms and every structure has at least one atom. `slots`: the 64 slot values of one atom are distinct and never equal 48. `validity`: an edge is valid only where its neighbour atom exists and belongs to the same structure.
All inputs are finite; a program needn't handle non-finite values.
Results may differ from the reference program's by a relative error of at most 0.0099.
Values may be sent and summed in bfloat16 or wider, within the bound.
A program may use at most 64 MiB of HBM per device.

```python
import jax
import jax.numpy as jnp
from jax import lax

C = 512
H = 512
Q = 128
K = 64
RIM = 48
A_DEV = 128
ATOMS = 2048
STRUCTS = 16
N_ATOM = 16


def layout(key):
    cut_key = jax.random.fold_in(key, 11)
    cuts = jax.random.permutation(cut_key, ATOMS - 1)[:STRUCTS - 1] + 1
    atom_index = jnp.arange(ATOMS, dtype=jnp.int32)
    owners = jnp.sum((atom_index[:, None] >= cuts[None, :]).astype(jnp.int32), axis=1).astype(jnp.int32)
    atom_keys = jax.random.split(jax.random.fold_in(key, 12), ATOMS)
    picks = jax.vmap(lambda single: jax.random.permutation(single, 2 * RIM)[:K])(atom_keys)
    slot_values = jnp.where(picks < RIM, picks, picks + 1).T.astype(jnp.int32)
    target = atom_index[None, :] + slot_values - RIM
    inside = (target >= 0) & (target < ATOMS)
    partner = owners[jnp.clip(target, 0, ATOMS - 1)]
    chance = jax.random.randint(jax.random.fold_in(key, 13), (K, ATOMS), 0, 1000)
    limit = 350 + 600 * atom_index // ATOMS
    valid = inside & (partner == owners[None, :]) & (chance < limit[None, :])
    return (owners, slot_values, valid.astype(jnp.int32))


def draw_struct_ids(key, part):
    return layout(key)[0]


def draw_slots(key, part):
    return layout(key)[1]


def draw_validity(key, part):
    return layout(key)[2]


def block_levels(rng, shape, cuts, low, high):
    factor_of = 1.0
    for axis_at, parts in cuts:
        heights = jax.random.uniform(jax.random.fold_in(jax.random.fold_in(rng, 6), axis_at), (parts,), jnp.float32, low / len(cuts), high / len(cuts))
        factor_of = factor_of * jnp.repeat(jnp.exp(heights), shape[axis_at] // parts).reshape((-1,) + (1,) * (len(shape) - 1 - axis_at))
    return factor_of


def scatter_about(own_key, shape, deviation, most, cuts=(), held_as=jnp.bfloat16):
    factor_of = block_levels(own_key, shape, cuts, -0.22, 0.18) if cuts else 1.0
    entries = jax.random.normal(own_key, shape, jnp.float32) * deviation * factor_of
    return jnp.minimum(jnp.maximum(entries, -most), most).astype(held_as)


def setup_inputs(seed: int = 0) -> dict:
    key_of = jax.random.split(jax.random.key(seed), 10)
    return {
        "positions": scatter_about(key_of[0], (3, ATOMS), 1.5, 9.0, ((1, 16),), jnp.float32),
        "features": scatter_about(key_of[1], (C, ATOMS), 1.0, 6.0, ((0, 2), (1, 16))),
        "struct_ids": draw_struct_ids(jax.random.fold_in(key_of[9], 71), 0),
        "slots": draw_slots(jax.random.fold_in(key_of[9], 71), 0),
        "validity": draw_validity(jax.random.fold_in(key_of[9], 71), 0),
        "radial_in": scatter_about(key_of[5], (H, Q), 12.0, 72.0),
        "radial_out": scatter_about(key_of[6], (C, H), (H * 128) ** -0.5, 0.0234375, ((0, 2),)),
        "mixing": scatter_about(key_of[7], (C, C), (C // 4) ** -0.5, 0.5, ((1, 2),)),
        "readout": scatter_about(key_of[8], (C,), (C * K * 16) ** -0.5, 0.0078125, (), jnp.float32),
    }


sharpness = 40.0
reach = 10.0

def dsilu(value):
    sigma = jax.nn.sigmoid(value)
    return sigma * (1.0 + value * (1.0 - sigma))

def radial_terms(vector, radial_in, radial_out):
    dist = jnp.sqrt(1.0 + lax.optimization_barrier(jnp.sum(vector * vector, axis=0)))
    count = radial_in.shape[1]
    centers = jnp.arange(count).astype(jnp.float32) * (reach / count)
    offset = dist[None, :] - centers[:, None]
    bump = jnp.exp(-sharpness * offset * offset)
    basis = bump.astype(jnp.bfloat16)
    slope = (-2.0 * sharpness * offset * bump).astype(jnp.bfloat16)
    pre = jnp.dot(radial_in, basis, preferred_element_type=jnp.float32)
    dpre = jnp.dot(radial_in, slope, preferred_element_type=jnp.float32)
    hidden = jax.nn.silu(pre).astype(jnp.bfloat16)
    dhidden = (dsilu(pre) * dpre).astype(jnp.bfloat16)
    radial = jnp.dot(radial_out, hidden, preferred_element_type=jnp.float32)
    dradial = jnp.dot(radial_out, dhidden, preferred_element_type=jnp.float32)
    return (dist, radial, dradial)

def reference(positions, features, struct_ids, slots, validity, radial_in, radial_out, mixing, readout):
    slot_count = slots.shape[0]

    def block_terms(block):
        start = (block * A_DEV).astype(jnp.int32)
        slot_block = lax.dynamic_slice_in_dim(slots, start, A_DEV, 1)
        valid_block = lax.dynamic_slice_in_dim(validity, start, A_DEV, 1).reshape(-1).astype(jnp.float32)
        atom_index = start + jnp.arange(A_DEV, dtype=jnp.int32)
        partner = jnp.clip(atom_index[None, :] + slot_block - RIM, 0, ATOMS - 1).astype(jnp.int32)
        own_pos = lax.dynamic_slice_in_dim(positions, start, A_DEV, 1)
        vector = (positions[:, partner] - own_pos[:, None, :]).reshape(3, -1)
        far_feat = features[:, partner].reshape(features.shape[0], -1)
        dist, radial, dradial = radial_terms(vector, radial_in, radial_out)
        message = (far_feat * radial).astype(jnp.bfloat16)
        mixed = jnp.dot(mixing, message, preferred_element_type=jnp.float32)
        gmix = (valid_block[None, :] * readout[:, None] * dsilu(mixed)).astype(jnp.bfloat16)
        gmsg = lax.dot_general(mixing, gmix, (((0,), (0,)), ((), ())), preferred_element_type=jnp.float32)
        gdist = lax.optimization_barrier(jnp.sum(gmsg * far_feat.astype(jnp.float32) * dradial, axis=0))
        gvec = gdist * vector / dist
        atomvir = (vector[:, None, :] * gvec[None, :, :]).reshape(9, slot_count, A_DEV).sum(axis=1)
        return (gvec.reshape(3, slot_count, A_DEV), atomvir)
    blocks = jnp.arange(N_ATOM, dtype=jnp.int32)
    gvecs, virs = lax.map(block_terms, blocks)
    gvec_all = jnp.transpose(gvecs, (1, 2, 0, 3)).reshape(3, slot_count, ATOMS)
    atomvir = jnp.transpose(virs, (1, 0, 2)).reshape(9, ATOMS)
    partner_all = jnp.clip(jnp.arange(ATOMS, dtype=jnp.int32)[None, :] + slots - RIM, 0, ATOMS - 1).astype(jnp.int32)
    incoming = jnp.zeros((3, ATOMS), jnp.float32).at[:, partner_all.reshape(-1)].add(-gvec_all.reshape(3, -1))
    forces = gvec_all.sum(axis=1) + incoming
    onehot = (struct_ids[None, :] == jnp.arange(STRUCTS, dtype=jnp.int32)[:, None]).astype(jnp.float32)
    virial = jnp.dot(atomvir, onehot.T, precision=lax.Precision.HIGHEST)
    counts = lax.optimization_barrier(jnp.sum(onehot, axis=1))
    stress = -virial / counts[None, :]
    return (forces, stress)
```

```python
import functools

import jax
import jax.numpy as jnp
from jax import lax
from jax.experimental import pallas as pl
from jax.experimental.pallas import tpu as pltpu
from jax.sharding import PartitionSpec as P

RIM = 48
sharpness = 40.0
reach = 10.0
F32 = jnp.float32
BF16 = jnp.bfloat16
TILE = 256
MESH = pl.DeviceIdType.MESH


def dot(a, b):
    return jnp.dot(a, b, preferred_element_type=F32)


def sigmoid(value):
    return 0.5 * jnp.tanh(0.5 * value) + 0.5


def kernel(
    size,
    structs,
    pos,
    feat,
    sid,
    slots,
    valid,
    r_in,
    r_out,
    mix,
    readout,
    forces,
    stress,
    fwin,
    pnbr,
    ro_r,
    mix_r,
    mix_t,
    pwin,
    own_pos,
    idx_s,
    w_s,
    hot_s,
    vec_s,
    dist_s,
    hid_s,
    dhid_s,
    mixp_s,
    fd_s,
    acc,
    gsum,
    avir,
    tab_own,
    tab_nbr,
    tabs,
    part,
    parts,
    total,
    totals,
    pos_sems,
    nbr_sems,
    own_sems,
    ro_sems,
    mix_sems,
    psems,
    tsems,
):
    a, c = lax.axis_index("atom"), lax.axis_index("chan")
    channels, atoms = feat.shape
    n = readout.shape[1] // channels
    half = atoms // n
    rows = slots.shape[0] // n
    group = 4 if size % 4 == 0 else 1
    deep = size // group
    place, z = lax.rem(a, group), lax.div(a, group)
    before, after = lax.rem(a + size - 1, size), lax.rem(a + 1, size)

    def at(atom, chan):
        return {"atom": atom, "chan": chan}

    plane = []
    for step in range(1, n * group):
        spot = lax.rem(place * n + c + step, n * group)
        plane.append((z * group + lax.div(spot, n), lax.rem(spot, n)))
    line = [(lax.rem(z + step, deep) * group + place, c) for step in range(1, deep)]
    ends = [(side, chan) for side in (before, after) for chan in range(n)]
    others = [(k, lax.rem(c + k, n)) for k in range(1, n)]
    early = c < n // 2

    barrier = pltpu.get_barrier_semaphore()
    for atom, chan in plane + line + ends:
        pl.semaphore_signal(barrier, inc=1, device_id=at(atom, chan), device_id_type=MESH)
    pl.semaphore_wait(barrier, len(plane) + len(line) + len(ends))

    def send(src, dst, sem, sem_recv, atom, chan):
        copy = pltpu.make_async_remote_copy(
            src_ref=src,
            dst_ref=dst,
            send_sem=sem,
            recv_sem=sem_recv,
            device_id=at(atom, chan),
            device_id_type=MESH,
        )
        copy.start()
        return copy

    nbr = pl.ds(atoms, atoms)
    own = pl.ds(0, atoms)
    started = [
        send(pos, pnbr, pos_sems.at[0], pos_sems.at[1], jnp.where(early, after, before), c)
    ]
    for chan in range(n):
        rel = lax.rem(c - chan + n, n)
        side = after if chan < n // 2 else before
        started.append(
            send(feat, fwin.at[rel, :, nbr], nbr_sems.at[0, chan], nbr_sems.at[1, rel], side, chan)
        )
    for k, chan in others:
        started.append(
            send(feat, fwin.at[n - k, :, own], own_sems.at[0, k], own_sems.at[1, n - k], a, chan)
        )
    for k, chan in others:
        started.append(send(r_out, ro_r.at[n - k - 1], ro_sems.at[0, k], ro_sems.at[1, n - k], a, chan))
        started.append(send(mix, mix_r.at[n - k - 1], mix_sems.at[0, k], mix_sems.at[1, n - k], a, chan))

    fwin[0, :, 0:atoms] = feat[...]
    lane = lax.broadcasted_iota(jnp.int32, (rows, atoms), 1)

    def fold(value):
        out = value[0:rows, :]
        for q in range(n):
            moved = pltpu.roll(value[q * rows : (q + 1) * rows, :], lax.rem((q - c + n) * half, atoms), 1)
            out = jnp.where((lane >= q * half) & (lane < (q + 1) * half), moved, out)
        return out

    def whole(value):
        out = value
        for q in range(1, n):
            out = out + pltpu.roll(value, q * half, 1)
        return out

    atom_of = c * half + lax.rem(lane, half)
    idx_s[...] = lax.bitwise_and(fold(slots[...]) + atom_of - RIM, 2 * atoms - 1)
    w_s[...] = fold(valid[...]).astype(F32)
    lane8 = lax.broadcasted_iota(jnp.int32, (8, atoms), 1)
    mine = (lane8 >= c * half) & (lane8 < c * half + half)
    own_pos[...] = jnp.zeros_like(own_pos)
    own_pos[0:3, :] = pos[...]
    spread = own_pos[...]
    pwin[...] = jnp.zeros_like(pwin)

    def split(value, columns):
        one = value.astype(BF16).astype(F32)
        two = (value - one).astype(BF16).astype(F32)
        pwin[0:3, columns] = one
        pwin[8:11, columns] = two
        pwin[16:19, columns] = value - one - two

    split(pos[...], slice(0, atoms))
    own_pos[...] = whole(jnp.where(mine, spread, 0.0))
    scale = readout[...]
    mix_t[0:channels, :] = (mix[...].astype(F32).T * scale).astype(BF16)
    acc[...] = jnp.zeros_like(acc)
    gsum[...] = jnp.zeros_like(gsum)
    avir[...] = jnp.zeros_like(avir)

    def landed(dst, sem):
        pltpu.make_async_copy(dst, dst, sem).wait()

    landed(pnbr, pos_sems.at[1])
    landed(fwin.at[0, :, nbr], nbr_sems.at[1, 0])
    split(pnbr[...], slice(atoms, 2 * atoms))
    count = r_in.shape[1]
    wide = TILE // atoms
    own_tile = jnp.concatenate([own_pos[...]] * wide, axis=1)
    steps = rows // wide

    def row(ref, step):
        return jnp.concatenate(
            [ref[pl.ds(step * wide + k, 1), :] for k in range(wide)], axis=1
        )

    def first(step, carry):
        idx = row(idx_s, step)
        spot = lax.broadcasted_iota(jnp.int32, (2 * atoms, TILE), 0)
        hot = jnp.where(spot == idx, 1.0, 0.0).astype(BF16)
        hot_s[step] = hot
        got = dot(pwin[...].astype(BF16), hot)
        vec = got[0:8] + got[8:16] + got[16:24] - own_tile
        vec_s[step] = vec
        dist = jnp.sqrt(1.0 + jnp.sum(vec * vec, axis=0, keepdims=True))
        dist_s[step] = dist
        centers = lax.broadcasted_iota(jnp.int32, (count, TILE), 0).astype(F32) * (reach / count)
        offset = dist - centers
        bump = jnp.exp(-sharpness * offset * offset)
        basis = bump.astype(BF16)
        slope = (-2.0 * sharpness * offset * bump).astype(BF16)
        pre = dot(r_in[...], basis)
        dpre = dot(r_in[...], slope)
        sigma = sigmoid(pre)
        silu = pre * sigma
        hid = silu.astype(BF16)
        dhid = ((sigma + silu * (1.0 - sigma)) * dpre).astype(BF16)
        hid_s[step] = hid
        dhid_s[step] = dhid
        far = dot(fwin[0], hot)
        message = (far * dot(r_out[...], hid)).astype(BF16)
        fd_s[step] = far * dot(r_out[...], dhid)
        mixp_s[step] = dot(mix[...], message)
        return carry

    lax.fori_loop(0, steps, first, 0)

    for r in range(1, n):
        landed(fwin.at[r, :, nbr], nbr_sems.at[1, r])
        landed(fwin.at[r, :, own], own_sems.at[1, r])
        landed(ro_r.at[r - 1], ro_sems.at[1, r])
        landed(mix_r.at[r - 1], mix_sems.at[1, r])
        mix_t[r * channels : (r + 1) * channels, :] = (
            mix_r[r - 1].astype(F32).T * scale
        ).astype(BF16)
    distant = (n - 1) * channels

    def second(step, carry):
        hot = hot_s[step]
        far = dot(fwin[1:].reshape(distant, 2 * atoms), hot)
        outer = ro_r[...].reshape(distant, ro_r.shape[2])
        message = (far * dot(outer, hid_s[step])).astype(BF16)
        fd = far * dot(outer, dhid_s[step])
        mixed = mixp_s[step]
        for r in range(1, n):
            mixed = mixed + dot(mix_r[r - 1], message[(r - 1) * channels : r * channels])
        sigma = sigmoid(mixed)
        gmix = (sigma + mixed * sigma * (1.0 - sigma)).astype(BF16)
        gmsg = dot(mix_t[...], gmix)
        gdist = jnp.sum(gmsg[0:channels] * fd_s[step], axis=0, keepdims=True) + jnp.sum(
            gmsg[channels:] * fd, axis=0, keepdims=True
        )
        vec = vec_s[step]
        gvec = (row(w_s, step) * gdist / dist_s[step]) * vec
        coarse = gvec.astype(BF16).astype(F32)
        both = jnp.concatenate([coarse, gvec - coarse], axis=0).astype(BF16)
        acc[...] += lax.dot_general(
            both, hot, (((1,), (1,)), ((), ())), preferred_element_type=F32
        )
        sums = gvec[:, 0:atoms]
        for k in range(1, wide):
            sums = sums + gvec[:, k * atoms : (k + 1) * atoms]
        gsum[...] += sums
        for p in range(3):
            term = vec[p : p + 1, :] * gvec
            sums = term[:, 0:atoms]
            for k in range(1, wide):
                sums = sums + term[:, k * atoms : (k + 1) * atoms]
            avir[8 * p : 8 * p + 8, :] += sums
        return carry

    lax.fori_loop(0, steps, second, 0)

    table = acc[0:8, :] + acc[8:16, :]
    tab_own[...] = jnp.where(mine, whole(gsum[...]), 0.0) - table[:, 0:atoms]
    tab_nbr[...] = -table[:, atoms : 2 * atoms]
    side = jnp.where(early, before, after)
    sends = []
    for k, chan in others:
        sends.append(send(tab_own, tabs.at[c], tsems.at[0, k], tsems.at[1, c], a, chan))
    for chan in range(n):
        sends.append(send(tab_nbr, tabs.at[n + c], tsems.at[2, chan], tsems.at[3, c], side, chan))
    tabs[c] = tab_own[...]
    spot = lax.broadcasted_iota(jnp.int32, (atoms, atoms), 0)
    member = jnp.where(spot == sid[...], 1.0, 0.0)
    ones = jnp.where(mine, 1.0, 0.0)
    local = jnp.concatenate([jnp.where(mine, whole(avir[8 * p : 8 * p + 8, :]), 0.0) for p in range(3)] + [ones], axis=0)
    virial = lax.dot_general(
        local, member, (((1,), (1,)), ((), ())), precision=lax.Precision.HIGHEST, preferred_element_type=F32
    )
    part[...] = jnp.zeros_like(part)
    for p in range(4):
        part[3 * p : 3 * p + 3, :] = virial[8 * p : 8 * p + 3, :]
    me = place * n + c
    for k, (atom, chan) in enumerate(plane):
        sends.append(send(part, parts.at[me], psems.at[0, k], psems.at[1, me], atom, chan))
    parts[me] = part[...]
    for k in range(1, n * group):
        spot = lax.rem(me + k, n * group)
        landed(parts.at[spot], psems.at[1, spot])
    summed = parts[0]
    for k in range(1, n * group):
        summed = summed + parts[k]
    total[...] = summed
    for k, (atom, chan) in enumerate(line):
        sends.append(send(total, totals.at[z], psems.at[2, k], psems.at[3, z], atom, chan))
    totals[z] = summed

    for k, chan in others:
        landed(tabs.at[chan], tsems.at[1, chan])
    for chan in range(n):
        landed(tabs.at[n + chan], tsems.at[3, chan])
    force = tabs[0]
    for k in range(1, 2 * n):
        force = force + tabs[k]
    forces[...] = force[0:3, :]

    for k in range(1, deep):
        spot = lax.rem(z + k, deep)
        landed(totals.at[spot], psems.at[3, spot])
    summed = totals[0]
    for k in range(1, deep):
        summed = summed + totals[k]
    out = -summed[0:9, :] / summed[9:10, :]
    stress[...] = out[:, 0:structs]
    for copy in (*started, *sends):
        copy.wait_send()


def local(positions, features, struct_ids, slots, validity, radial_in, radial_out, mixing, readout):
    size = lax.axis_size("atom")
    slot_count, atoms = slots.shape
    structs = atoms * size // 128
    channels, hidden = radial_out.shape
    group = 4 if size % 4 == 0 else 1
    deep = size // group
    n = lax.axis_size("chan")
    steps = slot_count * atoms // n // TILE
    plane = n * group
    vmem = pltpu.VMEM
    dma = pltpu.SemaphoreType.DMA
    return pl.pallas_call(
        functools.partial(kernel, size, structs),
        out_shape=(
            jax.ShapeDtypeStruct((3, atoms), F32),
            jax.ShapeDtypeStruct((9, structs), F32),
        ),
        in_specs=[pl.BlockSpec(memory_space=vmem)] * 9,
        out_specs=(pl.BlockSpec(memory_space=vmem),) * 2,
        scratch_shapes=[
            vmem((n, channels, 2 * atoms), BF16),
            vmem((3, atoms), F32),
            vmem((n - 1, channels, hidden), BF16),
            vmem((n - 1, n * channels, channels), BF16),
            vmem((n * channels, n * channels), BF16),
            vmem((32, 2 * atoms), F32),
            vmem((8, atoms), F32),
            vmem((slot_count // n, atoms), jnp.int32),
            vmem((slot_count // n, atoms), F32),
            vmem((steps, 2 * atoms, TILE), BF16),
            vmem((steps, 8, TILE), F32),
            vmem((steps, 1, TILE), F32),
            vmem((steps, hidden, TILE), BF16),
            vmem((steps, hidden, TILE), BF16),
            vmem((steps, n * channels, TILE), F32),
            vmem((steps, channels, TILE), F32),
            vmem((16, 2 * atoms), F32),
            vmem((8, atoms), F32),
            vmem((24, atoms), F32),
            vmem((8, atoms), F32),
            vmem((8, atoms), F32),
            vmem((2 * n, 8, atoms), F32),
            vmem((16, atoms), F32),
            vmem((plane, 16, atoms), F32),
            vmem((16, atoms), F32),
            vmem((deep, 16, atoms), F32),
            dma((2,)),
            dma((2, n)),
            dma((2, n)),
            dma((2, n)),
            dma((2, n)),
            dma((4, max(plane, deep))),
            dma((4, n)),
        ],
        compiler_params=pltpu.CompilerParams(
            collective_id=0, has_side_effects=True, vmem_limit_bytes=60 * 1024 * 1024
        ),
    )(
        positions,
        features,
        struct_ids.reshape(1, atoms),
        slots,
        validity,
        radial_in,
        radial_out,
        mixing,
        readout.reshape(1, n * channels),
    )


def solution(mesh):
    placed = (
        P(None, "atom"),
        P("chan", "atom"),
        P("atom"),
        P(None, "atom"),
        P(None, "atom"),
        P(),
        P("chan", None),
        P(None, "chan"),
        P(),
    )
    return jax.shard_map(
        local, mesh=mesh, in_specs=placed, out_specs=(P(None, "atom"), P()), check_vma=False
    )
```

```python
import functools

import jax
import jax.numpy as jnp
from jax import lax
from jax.experimental import pallas as pl
from jax.experimental.pallas import tpu as pltpu
from jax.sharding import PartitionSpec as P

RIM = 48
sharpness = 40.0
reach = 10.0
F32 = jnp.float32
BF16 = jnp.bfloat16
TILE = 512
MESH = pl.DeviceIdType.MESH


def dot(a, b):
    return jnp.dot(a, b, preferred_element_type=F32)


def sigmoid(value):
    return 0.5 * jnp.tanh(0.5 * value) + 0.5


def kernel(
    size,
    structs,
    pos,
    feat,
    sid,
    slots,
    valid,
    r_in,
    r_out,
    mix,
    readout,
    forces,
    stress,
    fwin,
    pnbr,
    ro_r,
    mix_r,
    mix_t,
    pwin,
    own_pos,
    idx_s,
    w_s,
    hot_s,
    vec_s,
    dist_s,
    hid_s,
    dhid_s,
    mixp_s,
    fd_s,
    acc,
    gsum,
    avir,
    tab_own,
    tab_nbr,
    tabs,
    part,
    parts,
    total,
    totals,
    pos_sems,
    nbr_sems,
    own_sems,
    ro_sems,
    mix_sems,
    psems,
    tsems,
):
    a, c = lax.axis_index("atom"), lax.axis_index("chan")
    channels, atoms = feat.shape
    n = readout.shape[1] // channels
    half = atoms // n
    rows = slots.shape[0] // n
    group = 4 if size % 4 == 0 else 1
    deep = size // group
    place, z = lax.rem(a, group), lax.div(a, group)
    before, after = lax.rem(a + size - 1, size), lax.rem(a + 1, size)

    def at(atom, chan):
        return {"atom": atom, "chan": chan}

    plane = []
    for step in range(1, n * group):
        spot = lax.rem(place * n + c + step, n * group)
        plane.append((z * group + lax.div(spot, n), lax.rem(spot, n)))
    line = [(lax.rem(z + step, deep) * group + place, c) for step in range(1, deep)]
    ends = [(side, chan) for side in (before, after) for chan in range(n)]
    others = [(k, lax.rem(c + k, n)) for k in range(1, n)]
    early = c < n // 2

    barrier = pltpu.get_barrier_semaphore()
    for atom, chan in plane + line + ends:
        pl.semaphore_signal(barrier, inc=1, device_id=at(atom, chan), device_id_type=MESH)
    pl.semaphore_wait(barrier, len(plane) + len(line) + len(ends))

    def send(src, dst, sem, sem_recv, atom, chan):
        copy = pltpu.make_async_remote_copy(
            src_ref=src,
            dst_ref=dst,
            send_sem=sem,
            recv_sem=sem_recv,
            device_id=at(atom, chan),
            device_id_type=MESH,
        )
        copy.start()
        return copy

    nbr = pl.ds(atoms, atoms)
    own = pl.ds(0, atoms)
    started = [
        send(pos, pnbr, pos_sems.at[0], pos_sems.at[1], jnp.where(early, after, before), c)
    ]
    for chan in range(n):
        rel = lax.rem(c - chan + n, n)
        side = after if chan < n // 2 else before
        started.append(
            send(feat, fwin.at[rel, :, nbr], nbr_sems.at[0, chan], nbr_sems.at[1, rel], side, chan)
        )
    for k, chan in others:
        started.append(
            send(feat, fwin.at[n - k, :, own], own_sems.at[0, k], own_sems.at[1, n - k], a, chan)
        )
    for k, chan in others:
        started.append(send(r_out, ro_r.at[n - k - 1], ro_sems.at[0, k], ro_sems.at[1, n - k], a, chan))
        started.append(send(mix, mix_r.at[n - k - 1], mix_sems.at[0, k], mix_sems.at[1, n - k], a, chan))

    fwin[0, :, 0:atoms] = feat[...]
    lane = lax.broadcasted_iota(jnp.int32, (rows, atoms), 1)

    def fold(value):
        out = value[0:rows, :]
        for q in range(n):
            moved = pltpu.roll(value[q * rows : (q + 1) * rows, :], lax.rem((q - c + n) * half, atoms), 1)
            out = jnp.where((lane >= q * half) & (lane < (q + 1) * half), moved, out)
        return out

    def whole(value):
        out = value
        for q in range(1, n):
            out = out + pltpu.roll(value, q * half, 1)
        return out

    atom_of = c * half + lax.rem(lane, half)
    idx_s[...] = lax.bitwise_and(fold(slots[...]) + atom_of - RIM, 2 * atoms - 1)
    w_s[...] = fold(valid[...]).astype(F32)
    lane8 = lax.broadcasted_iota(jnp.int32, (8, atoms), 1)
    mine = (lane8 >= c * half) & (lane8 < c * half + half)
    own_pos[...] = jnp.zeros_like(own_pos)
    own_pos[0:3, :] = pos[...]
    spread = own_pos[...]
    pwin[...] = jnp.zeros_like(pwin)

    def split(value, columns):
        one = value.astype(BF16).astype(F32)
        two = (value - one).astype(BF16).astype(F32)
        pwin[0:3, columns] = one
        pwin[8:11, columns] = two
        pwin[16:19, columns] = value - one - two

    split(pos[...], slice(0, atoms))
    own_pos[...] = whole(jnp.where(mine, spread, 0.0))
    scale = readout[...]
    mix_t[0:channels, :] = (mix[...].astype(F32).T * scale).astype(BF16)
    acc[...] = jnp.zeros_like(acc)
    gsum[...] = jnp.zeros_like(gsum)
    avir[...] = jnp.zeros_like(avir)

    def landed(dst, sem):
        pltpu.make_async_copy(dst, dst, sem).wait()

    landed(pnbr, pos_sems.at[1])
    landed(fwin.at[0, :, nbr], nbr_sems.at[1, 0])
    split(pnbr[...], slice(atoms, 2 * atoms))
    count = r_in.shape[1]
    wide = TILE // atoms
    own_tile = jnp.concatenate([own_pos[...]] * wide, axis=1)
    steps = rows // wide

    def row(ref, step):
        return jnp.concatenate(
            [ref[pl.ds(step * wide + k, 1), :] for k in range(wide)], axis=1
        )

    def first(step, carry):
        idx = row(idx_s, step)
        spot = lax.broadcasted_iota(jnp.int32, (2 * atoms, TILE), 0)
        hot = jnp.where(spot == idx, 1.0, 0.0).astype(BF16)
        hot_s[step] = hot
        got = dot(pwin[...].astype(BF16), hot)
        vec = got[0:8] + got[8:16] + got[16:24] - own_tile
        vec_s[step] = vec
        dist = jnp.sqrt(1.0 + jnp.sum(vec * vec, axis=0, keepdims=True))
        dist_s[step] = dist
        centers = lax.broadcasted_iota(jnp.int32, (count, TILE), 0).astype(F32) * (reach / count)
        offset = dist - centers
        bump = jnp.exp(-sharpness * offset * offset)
        basis = bump.astype(BF16)
        slope = (-2.0 * sharpness * offset * bump).astype(BF16)
        pre = dot(r_in[...], basis)
        dpre = dot(r_in[...], slope)
        sigma = sigmoid(pre)
        silu = pre * sigma
        hid = silu.astype(BF16)
        dhid = ((sigma + silu * (1.0 - sigma)) * dpre).astype(BF16)
        hid_s[step] = hid
        dhid_s[step] = dhid
        far = dot(fwin[0], hot)
        message = (far * dot(r_out[...], hid)).astype(BF16)
        fd_s[step] = far * dot(r_out[...], dhid)
        mixp_s[step] = dot(mix[...], message)
        return carry

    lax.fori_loop(0, steps, first, 0)

    for r in range(1, n):
        landed(fwin.at[r, :, nbr], nbr_sems.at[1, r])
        landed(fwin.at[r, :, own], own_sems.at[1, r])
        landed(ro_r.at[r - 1], ro_sems.at[1, r])
        landed(mix_r.at[r - 1], mix_sems.at[1, r])
        mix_t[r * channels : (r + 1) * channels, :] = (
            mix_r[r - 1].astype(F32).T * scale
        ).astype(BF16)
    distant = (n - 1) * channels

    def second(step, carry):
        hot = hot_s[step]
        far = dot(fwin[1:].reshape(distant, 2 * atoms), hot)
        outer = ro_r[...].reshape(distant, ro_r.shape[2])
        message = (far * dot(outer, hid_s[step])).astype(BF16)
        fd = far * dot(outer, dhid_s[step])
        mixed = mixp_s[step]
        for r in range(1, n):
            mixed = mixed + dot(mix_r[r - 1], message[(r - 1) * channels : r * channels])
        sigma = sigmoid(mixed)
        gmix = (sigma + mixed * sigma * (1.0 - sigma)).astype(BF16)
        gmsg = dot(mix_t[...], gmix)
        gdist = jnp.sum(gmsg[0:channels] * fd_s[step], axis=0, keepdims=True) + jnp.sum(
            gmsg[channels:] * fd, axis=0, keepdims=True
        )
        vec = vec_s[step]
        gvec = (row(w_s, step) * gdist / dist_s[step]) * vec
        coarse = gvec.astype(BF16).astype(F32)
        both = jnp.concatenate([coarse, gvec - coarse], axis=0).astype(BF16)
        acc[...] += lax.dot_general(
            both, hot, (((1,), (1,)), ((), ())), preferred_element_type=F32
        )
        sums = gvec[:, 0:atoms]
        for k in range(1, wide):
            sums = sums + gvec[:, k * atoms : (k + 1) * atoms]
        gsum[...] += sums
        for p in range(3):
            term = vec[p : p + 1, :] * gvec
            sums = term[:, 0:atoms]
            for k in range(1, wide):
                sums = sums + term[:, k * atoms : (k + 1) * atoms]
            avir[8 * p : 8 * p + 8, :] += sums
        return carry

    lax.fori_loop(0, steps, second, 0)

    table = acc[0:8, :] + acc[8:16, :]
    tab_own[...] = jnp.where(mine, whole(gsum[...]), 0.0) - table[:, 0:atoms]
    tab_nbr[...] = -table[:, atoms : 2 * atoms]
    side = jnp.where(early, before, after)
    sends = []
    for k, chan in others:
        sends.append(send(tab_own, tabs.at[c], tsems.at[0, k], tsems.at[1, c], a, chan))
    for chan in range(n):
        sends.append(send(tab_nbr, tabs.at[n + c], tsems.at[2, chan], tsems.at[3, c], side, chan))
    tabs[c] = tab_own[...]
    spot = lax.broadcasted_iota(jnp.int32, (atoms, atoms), 0)
    member = jnp.where(spot == sid[...], 1.0, 0.0)
    ones = jnp.where(mine, 1.0, 0.0)
    local = jnp.concatenate([jnp.where(mine, whole(avir[8 * p : 8 * p + 8, :]), 0.0) for p in range(3)] + [ones], axis=0)
    virial = lax.dot_general(
        local, member, (((1,), (1,)), ((), ())), precision=lax.Precision.HIGHEST, preferred_element_type=F32
    )
    part[...] = jnp.zeros_like(part)
    for p in range(4):
        part[3 * p : 3 * p + 3, :] = virial[8 * p : 8 * p + 3, :]
    me = place * n + c
    for k, (atom, chan) in enumerate(plane):
        sends.append(send(part, parts.at[me], psems.at[0, k], psems.at[1, me], atom, chan))
    parts[me] = part[...]
    for k in range(1, n * group):
        spot = lax.rem(me + k, n * group)
        landed(parts.at[spot], psems.at[1, spot])
    summed = parts[0]
    for k in range(1, n * group):
        summed = summed + parts[k]
    total[...] = summed
    for k, (atom, chan) in enumerate(line):
        sends.append(send(total, totals.at[z], psems.at[2, k], psems.at[3, z], atom, chan))
    totals[z] = summed

    for k, chan in others:
        landed(tabs.at[chan], tsems.at[1, chan])
    for chan in range(n):
        landed(tabs.at[n + chan], tsems.at[3, chan])
    force = tabs[0]
    for k in range(1, 2 * n):
        force = force + tabs[k]
    forces[...] = force[0:3, :]

    for k in range(1, deep):
        spot = lax.rem(z + k, deep)
        landed(totals.at[spot], psems.at[3, spot])
    summed = totals[0]
    for k in range(1, deep):
        summed = summed + totals[k]
    out = -summed[0:9, :] / summed[9:10, :]
    stress[...] = out[:, 0:structs]
    for copy in (*started, *sends):
        copy.wait_send()


def local(positions, features, struct_ids, slots, validity, radial_in, radial_out, mixing, readout):
    size = lax.axis_size("atom")
    slot_count, atoms = slots.shape
    structs = atoms * size // 128
    channels, hidden = radial_out.shape
    group = 4 if size % 4 == 0 else 1
    deep = size // group
    n = lax.axis_size("chan")
    steps = slot_count * atoms // n // TILE
    plane = n * group
    vmem = pltpu.VMEM
    dma = pltpu.SemaphoreType.DMA
    return pl.pallas_call(
        functools.partial(kernel, size, structs),
        out_shape=(
            jax.ShapeDtypeStruct((3, atoms), F32),
            jax.ShapeDtypeStruct((9, structs), F32),
        ),
        in_specs=[pl.BlockSpec(memory_space=vmem)] * 9,
        out_specs=(pl.BlockSpec(memory_space=vmem),) * 2,
        scratch_shapes=[
            vmem((n, channels, 2 * atoms), BF16),
            vmem((3, atoms), F32),
            vmem((n - 1, channels, hidden), BF16),
            vmem((n - 1, n * channels, channels), BF16),
            vmem((n * channels, n * channels), BF16),
            vmem((32, 2 * atoms), F32),
            vmem((8, atoms), F32),
            vmem((slot_count // n, atoms), jnp.int32),
            vmem((slot_count // n, atoms), F32),
            vmem((steps, 2 * atoms, TILE), BF16),
            vmem((steps, 8, TILE), F32),
            vmem((steps, 1, TILE), F32),
            vmem((steps, hidden, TILE), BF16),
            vmem((steps, hidden, TILE), BF16),
            vmem((steps, n * channels, TILE), F32),
            vmem((steps, channels, TILE), F32),
            vmem((16, 2 * atoms), F32),
            vmem((8, atoms), F32),
            vmem((24, atoms), F32),
            vmem((8, atoms), F32),
            vmem((8, atoms), F32),
            vmem((2 * n, 8, atoms), F32),
            vmem((16, atoms), F32),
            vmem((plane, 16, atoms), F32),
            vmem((16, atoms), F32),
            vmem((deep, 16, atoms), F32),
            dma((2,)),
            dma((2, n)),
            dma((2, n)),
            dma((2, n)),
            dma((2, n)),
            dma((4, max(plane, deep))),
            dma((4, n)),
        ],
        compiler_params=pltpu.CompilerParams(
            collective_id=0, has_side_effects=True, vmem_limit_bytes=60 * 1024 * 1024
        ),
    )(
        positions,
        features,
        struct_ids.reshape(1, atoms),
        slots,
        validity,
        radial_in,
        radial_out,
        mixing,
        readout.reshape(1, n * channels),
    )


def solution(mesh):
    placed = (
        P(None, "atom"),
        P("chan", "atom"),
        P("atom"),
        P(None, "atom"),
        P(None, "atom"),
        P(),
        P("chan", None),
        P(None, "chan"),
        P(),
    )
    return jax.shard_map(
        local, mesh=mesh, in_specs=placed, out_specs=(P(None, "atom"), P()), check_vma=False
    )
```

```python
import functools

import jax
import jax.numpy as jnp
from jax import lax
from jax.experimental import pallas as pl
from jax.experimental.pallas import tpu as pltpu
from jax.sharding import PartitionSpec as P

RIM = 48
sharpness = 40.0
reach = 10.0
F32 = jnp.float32
BF16 = jnp.bfloat16
TILE = 512
MESH = pl.DeviceIdType.MESH


def dot(a, b):
    return jnp.dot(a, b, preferred_element_type=F32)


def sigmoid(value):
    return 0.5 * jnp.tanh(0.5 * value) + 0.5


def kernel(
    size,
    structs,
    pos_h,
    feat_h,
    sid_h,
    slots_h,
    valid_h,
    r_in_h,
    r_out_h,
    mix_h,
    readout_h,
    forces,
    stress,
    pos,
    feat,
    sid,
    slots,
    valid,
    r_in,
    r_out,
    mix,
    readout,
    fwin,
    pnbr,
    ro_r,
    mix_r,
    mix_t,
    pwin,
    own_pos,
    idx_s,
    w_s,
    hot_s,
    vec_s,
    dist_s,
    hid_s,
    dhid_s,
    mixp_s,
    fd_s,
    acc,
    gsum,
    avir,
    tab_own,
    tab_nbr,
    tabs,
    part,
    parts,
    total,
    totals,
    pos_sems,
    nbr_sems,
    own_sems,
    ro_sems,
    mix_sems,
    psems,
    tsems,
    load_sems,
):
    a, c = lax.axis_index("atom"), lax.axis_index("chan")
    channels, atoms = feat.shape
    n = readout.shape[1] // channels
    half = atoms // n
    rows = slots.shape[0] // n
    group = 4 if size % 4 == 0 else 1
    deep = size // group
    place, z = lax.rem(a, group), lax.div(a, group)
    before, after = lax.rem(a + size - 1, size), lax.rem(a + 1, size)

    def at(atom, chan):
        return {"atom": atom, "chan": chan}

    plane = []
    for step in range(1, n * group):
        spot = lax.rem(place * n + c + step, n * group)
        plane.append((z * group + lax.div(spot, n), lax.rem(spot, n)))
    line = [(lax.rem(z + step, deep) * group + place, c) for step in range(1, deep)]
    ends = [(side, chan) for side in (before, after) for chan in range(n)]
    others = [(k, lax.rem(c + k, n)) for k in range(1, n)]
    early = c < n // 2

    barrier = pltpu.get_barrier_semaphore()
    for atom, chan in plane + line + ends:
        pl.semaphore_signal(barrier, inc=1, device_id=at(atom, chan), device_id_type=MESH)
    given = (pos_h, feat_h, slots_h, valid_h, mix_h, r_in_h, r_out_h, readout_h, sid_h)
    held = (pos, feat, slots, valid, mix, r_in, r_out, readout, sid)
    loads = [
        pltpu.make_async_copy(src, dst, load_sems.at[k]) for k, (src, dst) in enumerate(zip(given, held))
    ]
    for load in loads:
        load.start()
    pl.semaphore_wait(barrier, len(plane) + len(line) + len(ends))

    def send(src, dst, sem, sem_recv, atom, chan):
        copy = pltpu.make_async_remote_copy(
            src_ref=src,
            dst_ref=dst,
            send_sem=sem,
            recv_sem=sem_recv,
            device_id=at(atom, chan),
            device_id_type=MESH,
        )
        copy.start()
        return copy

    nbr = pl.ds(atoms, atoms)
    own = pl.ds(0, atoms)
    started = [
        send(pos_h, pnbr, pos_sems.at[0], pos_sems.at[1], jnp.where(early, after, before), c)
    ]
    for k in range(n):
        chan = lax.rem(c + k, n)
        rel = (n - k) % n
        side = jnp.where(chan < n // 2, after, before)
        started.append(
            send(feat_h, fwin.at[rel, :, nbr], nbr_sems.at[0, k], nbr_sems.at[1, rel], side, chan)
        )
    for k, chan in others:
        started.append(
            send(feat_h, fwin.at[n - k, :, own], own_sems.at[0, k], own_sems.at[1, n - k], a, chan)
        )
    for k, chan in others:
        started.append(send(r_out_h, ro_r.at[n - k - 1], ro_sems.at[0, k], ro_sems.at[1, n - k], a, chan))
        started.append(send(mix_h, mix_r.at[n - k - 1], mix_sems.at[0, k], mix_sems.at[1, n - k], a, chan))
    for load in loads:
        load.wait()

    fwin[0, :, 0:atoms] = feat[...]
    lane = lax.broadcasted_iota(jnp.int32, (rows, atoms), 1)

    def fold(value):
        out = value[0:rows, :]
        for q in range(n):
            moved = pltpu.roll(value[q * rows : (q + 1) * rows, :], lax.rem((q - c + n) * half, atoms), 1)
            out = jnp.where((lane >= q * half) & (lane < (q + 1) * half), moved, out)
        return out

    def whole(value):
        out = value
        for q in range(1, n):
            out = out + pltpu.roll(value, q * half, 1)
        return out

    atom_of = c * half + lax.rem(lane, half)
    idx_s[...] = lax.bitwise_and(fold(slots[...]) + atom_of - RIM, 2 * atoms - 1)
    w_s[...] = fold(valid[...]).astype(F32)
    lane8 = lax.broadcasted_iota(jnp.int32, (8, atoms), 1)
    mine = (lane8 >= c * half) & (lane8 < c * half + half)
    own_pos[...] = jnp.zeros_like(own_pos)
    own_pos[0:3, :] = pos[...]
    spread = own_pos[...]
    pwin[...] = jnp.zeros_like(pwin)

    def split(value, columns):
        one = value.astype(BF16).astype(F32)
        two = (value - one).astype(BF16).astype(F32)
        pwin[0:3, columns] = one
        pwin[8:11, columns] = two
        pwin[16:19, columns] = value - one - two

    split(pos[...], slice(0, atoms))
    own_pos[...] = whole(jnp.where(mine, spread, 0.0))
    scale = readout[...]
    mix_t[0:channels, :] = (mix[...].astype(F32).T * scale).astype(BF16)
    acc[...] = jnp.zeros_like(acc)
    gsum[...] = jnp.zeros_like(gsum)
    avir[...] = jnp.zeros_like(avir)

    def landed(dst, sem):
        pltpu.make_async_copy(dst, dst, sem).wait()

    landed(pnbr, pos_sems.at[1])
    landed(fwin.at[0, :, nbr], nbr_sems.at[1, 0])
    split(pnbr[...], slice(atoms, 2 * atoms))
    count = r_in.shape[1]
    wide = TILE // atoms
    own_tile = jnp.concatenate([own_pos[...]] * wide, axis=1)
    steps = rows // wide

    def row(ref, step):
        return jnp.concatenate(
            [ref[pl.ds(step * wide + k, 1), :] for k in range(wide)], axis=1
        )

    def first(step, carry):
        idx = row(idx_s, step)
        spot = lax.broadcasted_iota(jnp.int32, (2 * atoms, TILE), 0)
        hot = jnp.where(spot == idx, 1.0, 0.0).astype(BF16)
        hot_s[step] = hot
        got = dot(pwin[...].astype(BF16), hot)
        vec = got[0:8] + got[8:16] + got[16:24] - own_tile
        vec_s[step] = vec
        dist = jnp.sqrt(1.0 + jnp.sum(vec * vec, axis=0, keepdims=True))
        dist_s[step] = dist
        centers = lax.broadcasted_iota(jnp.int32, (count, TILE), 0).astype(F32) * (reach / count)
        offset = dist - centers
        bump = jnp.exp(-sharpness * offset * offset)
        basis = bump.astype(BF16)
        slope = (-2.0 * sharpness * offset * bump).astype(BF16)
        pre = dot(r_in[...], basis)
        dpre = dot(r_in[...], slope)
        sigma = sigmoid(pre)
        silu = pre * sigma
        hid = silu.astype(BF16)
        dhid = ((sigma + silu * (1.0 - sigma)) * dpre).astype(BF16)
        hid_s[step] = hid
        dhid_s[step] = dhid
        far = dot(fwin[0], hot)
        message = (far * dot(r_out[...], hid)).astype(BF16)
        fd_s[step] = far * dot(r_out[...], dhid)
        mixp_s[step] = dot(mix[...], message)
        return carry

    lax.fori_loop(0, steps, first, 0)

    for r in range(1, n):
        landed(fwin.at[r, :, nbr], nbr_sems.at[1, r])
        landed(fwin.at[r, :, own], own_sems.at[1, r])
        landed(ro_r.at[r - 1], ro_sems.at[1, r])
        landed(mix_r.at[r - 1], mix_sems.at[1, r])
        mix_t[r * channels : (r + 1) * channels, :] = (
            mix_r[r - 1].astype(F32).T * scale
        ).astype(BF16)
    distant = (n - 1) * channels

    def second(step, carry):
        hot = hot_s[step]
        far = dot(fwin[1:].reshape(distant, 2 * atoms), hot)
        outer = ro_r[...].reshape(distant, ro_r.shape[2])
        message = (far * dot(outer, hid_s[step])).astype(BF16)
        fd = far * dot(outer, dhid_s[step])
        mixed = mixp_s[step]
        for r in range(1, n):
            mixed = mixed + dot(mix_r[r - 1], message[(r - 1) * channels : r * channels])
        sigma = sigmoid(mixed)
        gmix = (sigma + mixed * sigma * (1.0 - sigma)).astype(BF16)
        gmsg = dot(mix_t[...], gmix)
        gdist = jnp.sum(gmsg[0:channels] * fd_s[step], axis=0, keepdims=True) + jnp.sum(
            gmsg[channels:] * fd, axis=0, keepdims=True
        )
        vec = vec_s[step]
        gvec = (row(w_s, step) * gdist / dist_s[step]) * vec
        coarse = gvec.astype(BF16).astype(F32)
        both = jnp.concatenate([coarse, gvec - coarse], axis=0).astype(BF16)
        acc[...] += lax.dot_general(
            both, hot, (((1,), (1,)), ((), ())), preferred_element_type=F32
        )
        sums = gvec[:, 0:atoms]
        for k in range(1, wide):
            sums = sums + gvec[:, k * atoms : (k + 1) * atoms]
        gsum[...] += sums
        for p in range(3):
            term = vec[p : p + 1, :] * gvec
            sums = term[:, 0:atoms]
            for k in range(1, wide):
                sums = sums + term[:, k * atoms : (k + 1) * atoms]
            avir[8 * p : 8 * p + 8, :] += sums
        return carry

    lax.fori_loop(0, steps, second, 0)

    table = acc[0:8, :] + acc[8:16, :]
    tab_own[...] = jnp.where(mine, whole(gsum[...]), 0.0) - table[:, 0:atoms]
    tab_nbr[...] = -table[:, atoms : 2 * atoms]
    side = jnp.where(early, before, after)
    sends = []
    for k, chan in others:
        sends.append(send(tab_own, tabs.at[c], tsems.at[0, k], tsems.at[1, c], a, chan))
    for chan in range(n):
        sends.append(send(tab_nbr, tabs.at[n + c], tsems.at[2, chan], tsems.at[3, c], side, chan))
    tabs[c] = tab_own[...]
    spot = lax.broadcasted_iota(jnp.int32, (atoms, atoms), 0)
    member = jnp.where(spot == sid[...], 1.0, 0.0)
    ones = jnp.where(mine, 1.0, 0.0)
    local = jnp.concatenate([jnp.where(mine, whole(avir[8 * p : 8 * p + 8, :]), 0.0) for p in range(3)] + [ones], axis=0)
    virial = lax.dot_general(
        local, member, (((1,), (1,)), ((), ())), precision=lax.Precision.HIGHEST, preferred_element_type=F32
    )
    part[...] = jnp.zeros_like(part)
    for p in range(4):
        part[3 * p : 3 * p + 3, :] = virial[8 * p : 8 * p + 3, :]
    me = place * n + c
    for k, (atom, chan) in enumerate(plane):
        sends.append(send(part, parts.at[me], psems.at[0, k], psems.at[1, me], atom, chan))
    parts[me] = part[...]
    for k in range(1, n * group):
        spot = lax.rem(me + k, n * group)
        landed(parts.at[spot], psems.at[1, spot])
    summed = parts[0]
    for k in range(1, n * group):
        summed = summed + parts[k]
    total[...] = summed
    for k, (atom, chan) in enumerate(line):
        sends.append(send(total, totals.at[z], psems.at[2, k], psems.at[3, z], atom, chan))
    totals[z] = summed

    for k, chan in others:
        landed(tabs.at[chan], tsems.at[1, chan])
    for chan in range(n):
        landed(tabs.at[n + chan], tsems.at[3, chan])
    force = tabs[0]
    for k in range(1, 2 * n):
        force = force + tabs[k]
    forces[...] = force[0:3, :]

    for k in range(1, deep):
        spot = lax.rem(z + k, deep)
        landed(totals.at[spot], psems.at[3, spot])
    summed = totals[0]
    for k in range(1, deep):
        summed = summed + totals[k]
    out = -summed[0:9, :] / summed[9:10, :]
    stress[...] = out[:, 0:structs]
    for copy in (*started, *sends):
        copy.wait_send()


def local(positions, features, struct_ids, slots, validity, radial_in, radial_out, mixing, readout):
    size = lax.axis_size("atom")
    slot_count, atoms = slots.shape
    structs = atoms * size // 128
    channels, hidden = radial_out.shape
    group = 4 if size % 4 == 0 else 1
    deep = size // group
    n = lax.axis_size("chan")
    steps = slot_count * atoms // n // TILE
    plane = n * group
    vmem = pltpu.VMEM
    dma = pltpu.SemaphoreType.DMA
    return pl.pallas_call(
        functools.partial(kernel, size, structs),
        out_shape=(
            jax.ShapeDtypeStruct((3, atoms), F32),
            jax.ShapeDtypeStruct((9, structs), F32),
        ),
        in_specs=[pl.BlockSpec(memory_space=pl.ANY)] * 9,
        out_specs=(pl.BlockSpec(memory_space=vmem),) * 2,
        scratch_shapes=[
            vmem((3, atoms), F32),
            vmem((channels, atoms), BF16),
            vmem((1, atoms), jnp.int32),
            vmem((slot_count, atoms), jnp.int32),
            vmem((slot_count, atoms), jnp.int32),
            vmem(radial_in.shape, BF16),
            vmem(radial_out.shape, BF16),
            vmem(mixing.shape, BF16),
            vmem((1, n * channels), F32),
            vmem((n, channels, 2 * atoms), BF16),
            vmem((3, atoms), F32),
            vmem((n - 1, channels, hidden), BF16),
            vmem((n - 1, n * channels, channels), BF16),
            vmem((n * channels, n * channels), BF16),
            vmem((32, 2 * atoms), F32),
            vmem((8, atoms), F32),
            vmem((slot_count // n, atoms), jnp.int32),
            vmem((slot_count // n, atoms), F32),
            vmem((steps, 2 * atoms, TILE), BF16),
            vmem((steps, 8, TILE), F32),
            vmem((steps, 1, TILE), F32),
            vmem((steps, hidden, TILE), BF16),
            vmem((steps, hidden, TILE), BF16),
            vmem((steps, n * channels, TILE), F32),
            vmem((steps, channels, TILE), F32),
            vmem((16, 2 * atoms), F32),
            vmem((8, atoms), F32),
            vmem((24, atoms), F32),
            vmem((8, atoms), F32),
            vmem((8, atoms), F32),
            vmem((2 * n, 8, atoms), F32),
            vmem((16, atoms), F32),
            vmem((plane, 16, atoms), F32),
            vmem((16, atoms), F32),
            vmem((deep, 16, atoms), F32),
            dma((2,)),
            dma((2, n)),
            dma((2, n)),
            dma((2, n)),
            dma((2, n)),
            dma((4, max(plane, deep))),
            dma((4, n)),
            dma((9,)),
        ],
        compiler_params=pltpu.CompilerParams(
            collective_id=0, has_side_effects=True, vmem_limit_bytes=60 * 1024 * 1024
        ),
    )(
        positions,
        features,
        struct_ids.reshape(1, atoms),
        slots,
        validity,
        radial_in,
        radial_out,
        mixing,
        readout.reshape(1, n * channels),
    )


def solution(mesh):
    placed = (
        P(None, "atom"),
        P("chan", "atom"),
        P("atom"),
        P(None, "atom"),
        P(None, "atom"),
        P(),
        P("chan", None),
        P(None, "chan"),
        P(),
    )
    return jax.shard_map(
        local, mesh=mesh, in_specs=placed, out_specs=(P(None, "atom"), P()), check_vma=False
    )
```

```python
import functools

import jax
import jax.numpy as jnp
from jax import lax
from jax.experimental import pallas as pl
from jax.experimental.pallas import tpu as pltpu
from jax.sharding import PartitionSpec as P

RIM = 48
sharpness = 40.0
reach = 10.0
F32 = jnp.float32
BF16 = jnp.bfloat16
TILE = 512
MESH = pl.DeviceIdType.MESH


def dot(a, b):
    return jnp.dot(a, b, preferred_element_type=F32)


def sigmoid(value):
    return 0.5 * jnp.tanh(0.5 * value) + 0.5


def kernel(
    size,
    pos_h,
    feat_h,
    sid_h,
    slots_h,
    valid_h,
    r_in_h,
    r_out_h,
    mix_h,
    readout_h,
    result,
    pos,
    feat,
    sid,
    slots,
    valid,
    r_in,
    r_out,
    mix,
    readout,
    fwin,
    pnbr,
    ro_r,
    mix_r,
    mix_t,
    pwin,
    own_pos,
    idx_s,
    w_s,
    hot_s,
    vec_s,
    dist_s,
    hid_s,
    dhid_s,
    mixp_s,
    fd_s,
    acc,
    gsum,
    avir,
    tab_own,
    tab_nbr,
    tabs,
    part,
    parts,
    total,
    totals,
    pos_sems,
    nbr_sems,
    own_sems,
    ro_sems,
    mix_sems,
    psems,
    tsems,
    load_sems,
):
    a, c = lax.axis_index("atom"), lax.axis_index("chan")
    channels, atoms = feat.shape
    n = readout.shape[1] // channels
    half = atoms // n
    rows = slots.shape[0] // n
    group = 4 if size % 4 == 0 else 1
    deep = size // group
    place, z = lax.rem(a, group), lax.div(a, group)
    before, after = lax.rem(a + size - 1, size), lax.rem(a + 1, size)

    def at(atom, chan):
        return {"atom": atom, "chan": chan}

    plane = []
    for step in range(1, n * group):
        spot = lax.rem(place * n + c + step, n * group)
        plane.append((z * group + lax.div(spot, n), lax.rem(spot, n)))
    line = [(lax.rem(z + step, deep) * group + place, c) for step in range(1, deep)]
    ends = [(side, chan) for side in (before, after) for chan in range(n)]
    others = [(k, lax.rem(c + k, n)) for k in range(1, n)]
    early = c < n // 2

    barrier = pltpu.get_barrier_semaphore()
    for atom, chan in plane + line + ends:
        pl.semaphore_signal(barrier, inc=1, device_id=at(atom, chan), device_id_type=MESH)
    given = (pos_h, feat_h, slots_h, valid_h, mix_h, r_in_h, r_out_h, readout_h, sid_h)
    held = (pos, feat, slots, valid, mix, r_in, r_out, readout, sid)
    loads = [
        pltpu.make_async_copy(src, dst, load_sems.at[k]) for k, (src, dst) in enumerate(zip(given, held))
    ]
    for load in loads:
        load.start()
    pl.semaphore_wait(barrier, len(plane) + len(line) + len(ends))

    def send(src, dst, sem, sem_recv, atom, chan):
        copy = pltpu.make_async_remote_copy(
            src_ref=src,
            dst_ref=dst,
            send_sem=sem,
            recv_sem=sem_recv,
            device_id=at(atom, chan),
            device_id_type=MESH,
        )
        copy.start()
        return copy

    nbr = pl.ds(atoms, atoms)
    own = pl.ds(0, atoms)
    started = [
        send(pos_h, pnbr, pos_sems.at[0], pos_sems.at[1], jnp.where(early, after, before), c)
    ]
    for k in range(n):
        chan = lax.rem(c + k, n)
        rel = (n - k) % n
        side = jnp.where(chan < n // 2, after, before)
        started.append(
            send(feat_h, fwin.at[rel, :, nbr], nbr_sems.at[0, k], nbr_sems.at[1, rel], side, chan)
        )
    for k, chan in others:
        started.append(
            send(feat_h, fwin.at[n - k, :, own], own_sems.at[0, k], own_sems.at[1, n - k], a, chan)
        )
    for k, chan in others:
        started.append(send(r_out_h, ro_r.at[n - k - 1], ro_sems.at[0, k], ro_sems.at[1, n - k], a, chan))
        started.append(send(mix_h, mix_r.at[n - k - 1], mix_sems.at[0, k], mix_sems.at[1, n - k], a, chan))
    for load in loads:
        load.wait()

    fwin[0, :, 0:atoms] = feat[...]
    lane = lax.broadcasted_iota(jnp.int32, (rows, atoms), 1)

    def fold(value):
        out = value[0:rows, :]
        for q in range(n):
            moved = pltpu.roll(value[q * rows : (q + 1) * rows, :], lax.rem((q - c + n) * half, atoms), 1)
            out = jnp.where((lane >= q * half) & (lane < (q + 1) * half), moved, out)
        return out

    def whole(value):
        out = value
        for q in range(1, n):
            out = out + pltpu.roll(value, q * half, 1)
        return out

    atom_of = c * half + lax.rem(lane, half)
    idx_s[...] = lax.bitwise_and(fold(slots[...]) + atom_of - RIM, 2 * atoms - 1)
    w_s[...] = fold(valid[...]).astype(F32)
    lane8 = lax.broadcasted_iota(jnp.int32, (8, atoms), 1)
    mine = (lane8 >= c * half) & (lane8 < c * half + half)
    own_pos[...] = jnp.zeros_like(own_pos)
    own_pos[0:3, :] = pos[...]
    spread = own_pos[...]
    pwin[...] = jnp.zeros_like(pwin)

    def split(value, columns):
        one = value.astype(BF16).astype(F32)
        two = (value - one).astype(BF16).astype(F32)
        pwin[0:3, columns] = one
        pwin[8:11, columns] = two
        pwin[16:19, columns] = value - one - two

    split(pos[...], slice(0, atoms))
    own_pos[...] = whole(jnp.where(mine, spread, 0.0))
    scale = readout[...]
    mix_t[0:channels, :] = (mix[...].astype(F32).T * scale).astype(BF16)
    acc[...] = jnp.zeros_like(acc)
    gsum[...] = jnp.zeros_like(gsum)
    avir[...] = jnp.zeros_like(avir)

    def landed(dst, sem):
        pltpu.make_async_copy(dst, dst, sem).wait()

    landed(pnbr, pos_sems.at[1])
    landed(fwin.at[0, :, nbr], nbr_sems.at[1, 0])
    split(pnbr[...], slice(atoms, 2 * atoms))
    count = r_in.shape[1]
    wide = TILE // atoms
    own_tile = jnp.concatenate([own_pos[...]] * wide, axis=1)
    steps = rows // wide

    def row(ref, step):
        return jnp.concatenate(
            [ref[pl.ds(step * wide + k, 1), :] for k in range(wide)], axis=1
        )

    def first(step, carry):
        idx = row(idx_s, step)
        spot = lax.broadcasted_iota(jnp.int32, (2 * atoms, TILE), 0)
        hot = jnp.where(spot == idx, 1.0, 0.0).astype(BF16)
        hot_s[step] = hot
        got = dot(pwin[...].astype(BF16), hot)
        vec = got[0:8] + got[8:16] + got[16:24] - own_tile
        vec_s[step] = vec
        dist = jnp.sqrt(1.0 + jnp.sum(vec * vec, axis=0, keepdims=True))
        dist_s[step] = dist
        centers = lax.broadcasted_iota(jnp.int32, (count, TILE), 0).astype(F32) * (reach / count)
        offset = dist - centers
        bump = jnp.exp(-sharpness * offset * offset)
        basis = bump.astype(BF16)
        slope = (-2.0 * sharpness * offset * bump).astype(BF16)
        pre = dot(r_in[...], basis)
        dpre = dot(r_in[...], slope)
        sigma = sigmoid(pre)
        silu = pre * sigma
        hid = silu.astype(BF16)
        dhid = ((sigma + silu * (1.0 - sigma)) * dpre).astype(BF16)
        hid_s[step] = hid
        dhid_s[step] = dhid
        far = dot(fwin[0], hot)
        message = (far * dot(r_out[...], hid)).astype(BF16)
        fd_s[step] = far * dot(r_out[...], dhid)
        mixp_s[step] = dot(mix[...], message)
        return carry

    lax.fori_loop(0, steps, first, 0)

    for r in range(1, n):
        landed(fwin.at[r, :, nbr], nbr_sems.at[1, r])
        landed(fwin.at[r, :, own], own_sems.at[1, r])
        landed(ro_r.at[r - 1], ro_sems.at[1, r])
        landed(mix_r.at[r - 1], mix_sems.at[1, r])
        mix_t[r * channels : (r + 1) * channels, :] = (
            mix_r[r - 1].astype(F32).T * scale
        ).astype(BF16)
    distant = (n - 1) * channels

    def second(step, carry):
        hot = hot_s[step]
        far = dot(fwin[1:].reshape(distant, 2 * atoms), hot)
        outer = ro_r[...].reshape(distant, ro_r.shape[2])
        message = (far * dot(outer, hid_s[step])).astype(BF16)
        fd = far * dot(outer, dhid_s[step])
        mixed = mixp_s[step]
        for r in range(1, n):
            mixed = mixed + dot(mix_r[r - 1], message[(r - 1) * channels : r * channels])
        sigma = sigmoid(mixed)
        gmix = (sigma + mixed * sigma * (1.0 - sigma)).astype(BF16)
        gmsg = dot(mix_t[...], gmix)
        gdist = jnp.sum(gmsg[0:channels] * fd_s[step], axis=0, keepdims=True) + jnp.sum(
            gmsg[channels:] * fd, axis=0, keepdims=True
        )
        vec = vec_s[step]
        gvec = (row(w_s, step) * gdist / dist_s[step]) * vec
        coarse = gvec.astype(BF16).astype(F32)
        both = jnp.concatenate([coarse, gvec - coarse], axis=0).astype(BF16)
        acc[...] += lax.dot_general(
            both, hot, (((1,), (1,)), ((), ())), preferred_element_type=F32
        )
        sums = gvec[:, 0:atoms]
        for k in range(1, wide):
            sums = sums + gvec[:, k * atoms : (k + 1) * atoms]
        gsum[...] += sums
        for p in range(3):
            term = vec[p : p + 1, :] * gvec
            sums = term[:, 0:atoms]
            for k in range(1, wide):
                sums = sums + term[:, k * atoms : (k + 1) * atoms]
            avir[8 * p : 8 * p + 8, :] += sums
        return carry

    lax.fori_loop(0, steps, second, 0)

    table = acc[0:8, :] + acc[8:16, :]
    tab_own[...] = jnp.where(mine, whole(gsum[...]), 0.0) - table[:, 0:atoms]
    tab_nbr[...] = -table[:, atoms : 2 * atoms]
    side = jnp.where(early, before, after)
    sends = []
    for k, chan in others:
        sends.append(send(tab_own, tabs.at[c], tsems.at[0, k], tsems.at[1, c], a, chan))
    for chan in range(n):
        sends.append(send(tab_nbr, tabs.at[n + c], tsems.at[2, chan], tsems.at[3, c], side, chan))
    tabs[c] = tab_own[...]
    spot = lax.broadcasted_iota(jnp.int32, (atoms, atoms), 0)
    member = jnp.where(spot == sid[...], 1.0, 0.0)
    ones = jnp.where(mine, 1.0, 0.0)
    local = jnp.concatenate([jnp.where(mine, whole(avir[8 * p : 8 * p + 8, :]), 0.0) for p in range(3)] + [ones], axis=0)
    virial = lax.dot_general(
        local, member, (((1,), (1,)), ((), ())), precision=lax.Precision.HIGHEST, preferred_element_type=F32
    )
    part[...] = jnp.zeros_like(part)
    for p in range(4):
        part[3 * p : 3 * p + 3, :] = virial[8 * p : 8 * p + 3, :]
    me = place * n + c
    for k, (atom, chan) in enumerate(plane):
        sends.append(send(part, parts.at[me], psems.at[0, k], psems.at[1, me], atom, chan))
    parts[me] = part[...]
    for k in range(1, n * group):
        spot = lax.rem(me + k, n * group)
        landed(parts.at[spot], psems.at[1, spot])
    summed = parts[0]
    for k in range(1, n * group):
        summed = summed + parts[k]
    total[...] = summed
    for k, (atom, chan) in enumerate(line):
        sends.append(send(total, totals.at[z], psems.at[2, k], psems.at[3, z], atom, chan))
    totals[z] = summed

    for k, chan in others:
        landed(tabs.at[chan], tsems.at[1, chan])
    for chan in range(n):
        landed(tabs.at[n + chan], tsems.at[3, chan])
    force = tabs[0]
    for k in range(1, 2 * n):
        force = force + tabs[k]
    result[0:8, :] = force

    for k in range(1, deep):
        spot = lax.rem(z + k, deep)
        landed(totals.at[spot], psems.at[3, spot])
    summed = totals[0]
    for k in range(1, deep):
        summed = summed + totals[k]
    result[8:24, :] = -summed / summed[9:10, :]
    for copy in (*started, *sends):
        copy.wait_send()


def unpack(result, forces, stress):
    forces[...] = result[0 : forces.shape[0], :]
    stress[...] = result[8 : 8 + stress.shape[0], 0 : stress.shape[1]]


def local(positions, features, struct_ids, slots, validity, radial_in, radial_out, mixing, readout):
    size = lax.axis_size("atom")
    slot_count, atoms = slots.shape
    structs = atoms * size // 128
    channels, hidden = radial_out.shape
    group = 4 if size % 4 == 0 else 1
    deep = size // group
    n = lax.axis_size("chan")
    steps = slot_count * atoms // n // TILE
    plane = n * group
    vmem = pltpu.VMEM
    dma = pltpu.SemaphoreType.DMA
    result = pl.pallas_call(
        functools.partial(kernel, size),
        out_shape=jax.ShapeDtypeStruct((24, atoms), F32),
        in_specs=[pl.BlockSpec(memory_space=pl.ANY)] * 9,
        out_specs=pl.BlockSpec(memory_space=vmem),
        scratch_shapes=[
            vmem((3, atoms), F32),
            vmem((channels, atoms), BF16),
            vmem((1, atoms), jnp.int32),
            vmem((slot_count, atoms), jnp.int32),
            vmem((slot_count, atoms), jnp.int32),
            vmem(radial_in.shape, BF16),
            vmem(radial_out.shape, BF16),
            vmem(mixing.shape, BF16),
            vmem((1, n * channels), F32),
            vmem((n, channels, 2 * atoms), BF16),
            vmem((3, atoms), F32),
            vmem((n - 1, channels, hidden), BF16),
            vmem((n - 1, n * channels, channels), BF16),
            vmem((n * channels, n * channels), BF16),
            vmem((32, 2 * atoms), F32),
            vmem((8, atoms), F32),
            vmem((slot_count // n, atoms), jnp.int32),
            vmem((slot_count // n, atoms), F32),
            vmem((steps, 2 * atoms, TILE), BF16),
            vmem((steps, 8, TILE), F32),
            vmem((steps, 1, TILE), F32),
            vmem((steps, hidden, TILE), BF16),
            vmem((steps, hidden, TILE), BF16),
            vmem((steps, n * channels, TILE), F32),
            vmem((steps, channels, TILE), F32),
            vmem((16, 2 * atoms), F32),
            vmem((8, atoms), F32),
            vmem((24, atoms), F32),
            vmem((8, atoms), F32),
            vmem((8, atoms), F32),
            vmem((2 * n, 8, atoms), F32),
            vmem((16, atoms), F32),
            vmem((plane, 16, atoms), F32),
            vmem((16, atoms), F32),
            vmem((deep, 16, atoms), F32),
            dma((2,)),
            dma((2, n)),
            dma((2, n)),
            dma((2, n)),
            dma((2, n)),
            dma((4, max(plane, deep))),
            dma((4, n)),
            dma((9,)),
        ],
        compiler_params=pltpu.CompilerParams(
            collective_id=0, has_side_effects=True, vmem_limit_bytes=60 * 1024 * 1024
        ),
    )(
        positions,
        features,
        struct_ids.reshape(1, atoms),
        slots,
        validity,
        radial_in,
        radial_out,
        mixing,
        readout.reshape(1, n * channels),
    )
    return pl.pallas_call(
        unpack,
        out_shape=(
            jax.ShapeDtypeStruct((3, atoms), F32),
            jax.ShapeDtypeStruct((9, structs), F32),
        ),
        in_specs=[pl.BlockSpec(memory_space=vmem)],
        out_specs=(pl.BlockSpec(memory_space=vmem),) * 2,
    )(result)


def solution(mesh):
    placed = (
        P(None, "atom"),
        P("chan", "atom"),
        P("atom"),
        P(None, "atom"),
        P(None, "atom"),
        P(),
        P("chan", None),
        P(None, "chan"),
        P(),
    )
    return jax.shard_map(
        local, mesh=mesh, in_specs=placed, out_specs=(P(None, "atom"), P()), check_vma=False
    )
```
